32 devices in a mesh: groups: 2 (over x), loop: 16 (over z, y, core).
Axes of the slice: x: 2, y: 2, z: 4, core: 2. Of those that a mesh axis runs over, the one named last changes fastest.
Arguments:
- queries: bfloat16 [256, 4, 64, 128], P(('groups', 'loop')), parts along dimension 0, may hold values from -16 to 16
- new_keys: bfloat16 [256, 4, 4, 128], P(('groups', 'loop')), parts along dimension 0, may hold values from -8 to 8
- new_values: bfloat16 [256, 4, 4, 128], P(('groups', 'loop')), parts along dimension 0, may hold values from -12 to 12
- suffix_keys: bfloat16 [256, 256, 4, 128], P(('groups', 'loop')), parts along dimension 0, may hold values from -8 to 8
- suffix_values: bfloat16 [256, 256, 4, 128], P(('groups', 'loop')), parts along dimension 0, may hold values from -12 to 12
- suffix_len: int32 [256], P(('groups', 'loop')), parts along dimension 0, may hold values from 1 to 256, 16384 in all
- prefix_keys: bfloat16 [32, 64, 4, 128], P(('groups', 'loop')), parts along dimension 0, may hold values from -8 to 8
- prefix_values: bfloat16 [32, 64, 4, 128], P(('groups', 'loop')), parts along dimension 0, may hold values from -12 to 12
- block_ids: int32 [32], P(('groups', 'loop')), parts along dimension 0, may hold values from 0 to 15, each once
- block_lists: int32 [256, 4], P(('groups', 'loop')), parts along dimension 0, may hold values from 0 to 15, all different within a row
Outputs:
- attended: bfloat16 [256, 4, 64, 128], P(('groups', 'loop')), parts along dimension 0
The draws below stay inside these ranges and needn't reach their ends.
There are 2 independent parts, one for each index of `groups`. The reference program is written for one: setup_inputs(seed, part) draws one part's arguments, and reference() takes and returns one part's arrays. A program takes and returns all parts, laid end to end along the dimension named above; each array names one. Nothing has to cross between parts.
Inputs may be any that keep to these rules, and one draw needn't show every extreme that they name: `block_ids`: each slot holds a different block. `block_lists`: each request names 4 different blocks; every block is named by some request. `suffix_len`: some request uses all 256 slots.
All inputs are finite; a program needn't handle non-finite values. No bound on the sum of `suffix_len` on one device may be relied on, other than what follows from the above.
Results may differ from the reference program's by a relative error of at most 0.004.
Values may be sent and summed in bfloat16 or wider, within the bound.
No kernel may reach another device: no remote copies, remote signals or barrier semaphores. Data moves between devices by JAX's collectives and lax.ppermute only.
A program may use at most 64 MiB of HBM per device.

```python
import math
import jax
import jax.numpy as jnp
import numpy as np
from jax import lax

SUF = 256
STEPS = 4
NBR = 4
BS = 64
HD = 128
QH = 64
KVH = 4
GROUP = 16
REQUESTS = 128
NBLK = 16


def joint_draw(key):
    folded = jax.random.fold_in(key, 17)
    key_query, key_fresh = jax.random.split(folded, 2)
    query_rows = jnp.clip(jax.random.normal(key_query, (REQUESTS, STEPS, QH, HD), jnp.float32), -6.0, 6.0)
    fresh_keys = jnp.clip(2.0 * jax.random.normal(key_fresh, (REQUESTS, STEPS, KVH, HD), jnp.float32), -8.0, 8.0)
    return (query_rows, fresh_keys)


def draw_queries(key, part):
    return joint_draw(key)[0].astype(jnp.bfloat16)


def draw_new_keys(key, part):
    return joint_draw(key)[1].astype(jnp.bfloat16)


def steps_of(stream_key, extent, cuts, least, top_value):
    level, own = 1.0, jax.random.fold_in(stream_key, 6)
    for dim, parts in cuts:
        steps = jnp.exp(jax.random.uniform(jax.random.fold_in(own, dim), (parts,), jnp.float32, least / len(cuts), top_value / len(cuts)))
        level = level * jnp.repeat(steps, extent[dim] // parts).reshape([-1 if axis == dim else 1 for axis in range(len(extent))])
    return level


def different_ones(rng, rows, number_of, top, lift):
    sequence = jax.random.permutation(jax.random.fold_in(rng, 1), number_of)
    favour = sequence
    for power in range(3):
        favour = favour * favour // number_of
    favour = favour * lift // number_of
    lots = jax.random.randint(jax.random.fold_in(rng, 2), (rows, number_of), 0, 4096) + favour
    holders = jax.random.permutation(jax.random.fold_in(rng, 3), rows)[jnp.arange(number_of) % rows]
    lots = jnp.where(jnp.arange(rows)[:, None] == holders[None, :], 1 << 14, lots)
    priority = lots * number_of + jnp.arange(number_of)
    return lax.top_k(priority.astype(jnp.int32), top)[1].astype(jnp.int32)


def length_profile(number_of, total, reach, slope):
    loads = [(1 << 20) // math.isqrt(standing ** slope) + 1 for standing in range(2, number_of + 1)]
    surplus, counts = total - reach - (number_of - 1), [1] * (number_of - 1)
    while surplus > 0:
        movable = [i for i in range(number_of - 1) if counts[i] < reach]
        pool, remaining = sum([loads[i] for i in movable]), surplus
        for i in movable:
            extra = min(reach - counts[i], max(1, remaining * loads[i] // pool), surplus)
            counts[i] = counts[i] + extra
            surplus = surplus - extra
    return np.array([reach] + counts)


def ragged_sizes(rng, number_of, total, bound, slope):
    if number_of == 2:
        one = jax.random.randint(rng, (), max(1, total - bound), min(bound, total - 1) + 1)
        return jnp.stack([one, total - one])
    tallies = jnp.asarray(length_profile(number_of, total, bound, slope), jnp.int32)
    twos = (number_of - 1) // 2
    source_of, sink = tallies[1:1 + 2 * twos:2], tallies[2:2 + 2 * twos:2]
    margin = jnp.minimum(source_of - 1, bound - sink)
    shifted = jax.random.randint(jax.random.fold_in(rng, 1), (twos,), 0, 1 << 20) % (margin + 1)
    tallies = tallies.at[1:1 + 2 * twos:2].set(source_of - shifted).at[2:2 + 2 * twos:2].set(sink + shifted)
    return tallies[jax.random.permutation(jax.random.fold_in(rng, 2), number_of)]


def scatter_about(rng, extent, scale, most, pieces=(), kind=jnp.bfloat16):
    result = scale * jax.random.normal(rng, extent, jnp.float32)
    if pieces:
        result = result * steps_of(rng, extent, pieces, -0.22, 0.18)
    return jnp.clip(result, -most, most).astype(kind)


def setup_inputs(seed: int = 0, part: int = 0) -> dict:
    keys = jax.random.split(jax.random.key(seed), 11)
    own_keys = jax.random.split(jax.random.fold_in(keys[10], part), 11)
    queries = draw_queries(jax.random.fold_in(jax.random.fold_in(keys[10], part), 71), part)
    new_keys = draw_new_keys(jax.random.fold_in(jax.random.fold_in(keys[10], part), 71), part)
    new_values = scatter_about(own_keys[2], (REQUESTS, STEPS, KVH, HD), 3.0, 12.0, ((0, 16),))
    suffix_keys = scatter_about(own_keys[3], (REQUESTS, SUF, KVH, HD), 2.0, 8.0, ((0, 16),))
    suffix_values = scatter_about(own_keys[4], (REQUESTS, SUF, KVH, HD), 3.0, 12.0, ((0, 16),))
    suffix_len = ragged_sizes(own_keys[5], REQUESTS, REQUESTS * SUF // 2, SUF, 2).astype(jnp.int32)
    prefix_keys = scatter_about(own_keys[6], (NBLK, BS, KVH, HD), 2.0, 8.0, ((0, 16),))
    prefix_values = scatter_about(own_keys[7], (NBLK, BS, KVH, HD), 3.0, 12.0, ((0, 16),))
    block_ids = jax.random.permutation(own_keys[8], NBLK).astype(jnp.int32)
    block_lists = different_ones(own_keys[9], REQUESTS, NBLK, NBR, 4096)
    return dict(queries=queries, new_keys=new_keys, new_values=new_values, suffix_keys=suffix_keys, suffix_values=suffix_values, suffix_len=suffix_len, prefix_keys=prefix_keys, prefix_values=prefix_values, block_ids=block_ids, block_lists=block_lists)


def reference(queries, new_keys, new_values, suffix_keys, suffix_values, suffix_len, prefix_keys, prefix_values, block_ids, block_lists):
    slot_of = jnp.zeros((NBLK,), jnp.int32).at[block_ids].set(jnp.arange(NBLK, dtype=jnp.int32))
    score_scale = 1.0 / math.sqrt(HD)
    prior_count = NBR * BS
    total_keys = prior_count + SUF + STEPS

    def one_request(packed):
        query_rows, fresh_keys, fresh_values, tail_keys, tail_values, tail_len, named = packed
        slots = slot_of[named].astype(jnp.int32)
        prior_keys = prefix_keys[slots].reshape(prior_count, KVH, HD)
        prior_values = prefix_values[slots].reshape(prior_count, KVH, HD)
        key_rows = jnp.concatenate([prior_keys, tail_keys, fresh_keys], axis=0).astype(jnp.float32)
        value_rows = jnp.concatenate([prior_values, tail_values, fresh_values], axis=0).astype(jnp.float32)
        position = jnp.arange(total_keys, dtype=jnp.int32)
        base_visible = (position < prior_count) | (position >= prior_count) & (position < prior_count + tail_len)
        fresh_index = position - prior_count - SUF
        step_index = jnp.arange(STEPS, dtype=jnp.int32)
        visible = base_visible[None, :] | (fresh_index[None, :] >= 0) & (fresh_index[None, :] <= step_index[:, None])
        expanded_keys = jnp.repeat(key_rows, GROUP, axis=1)
        expanded_values = jnp.repeat(value_rows, GROUP, axis=1)
        scores = jnp.einsum('shd,khd->shk', query_rows.astype(jnp.float32), expanded_keys) * score_scale
        shown = visible[:, None, :]
        row_top = lax.optimization_barrier(jnp.max(jnp.where(shown, scores, -jnp.inf), axis=-1, keepdims=True))
        weights = jnp.where(shown, jnp.exp(scores - row_top), 0.0)
        totals = lax.optimization_barrier(jnp.sum(weights, axis=-1))
        rounded = lax.optimization_barrier(weights.astype(jnp.bfloat16)).astype(jnp.float32)
        mixed = jnp.einsum('shk,khd->shd', rounded, expanded_values) / totals[..., None]
        return mixed.astype(jnp.bfloat16)
    return lax.map(one_request, (queries, new_keys, new_values, suffix_keys, suffix_values, suffix_len, block_lists))
```

```python
import functools
import math

import jax
import jax.numpy as jnp
from jax import lax
from jax.experimental import pallas as pl
from jax.experimental.pallas import tpu as pltpu
from jax.sharding import PartitionSpec as P


ID_ROWS = 16
NT = (((1,), (1,)), ((), ()))


def ring_of_chips(chips):
    inner = 1 << ((chips.bit_length() - 1) // 2)
    outer = chips // inner
    if inner == 1 or outer % 2:
        return list(range(chips))
    walk = [(a, 0) for a in range(outer)]
    for step, a in enumerate(reversed(range(outer))):
        row = [(a, b) for b in range(1, inner)]
        walk += row if step % 2 == 0 else row[::-1]
    return [a * inner + b for a, b in walk]


def pack_kernel(id_ref, k_ref, v_ref, out_ref, scratch, *, heads, block):
    number = id_ref[0]
    high, low = number // 256, number % 256
    row = lax.broadcasted_iota(jnp.int32, (ID_ROWS, out_ref.shape[1]), 0)
    tag = jnp.where(row < ID_ROWS // 2, high, low)
    out_ref[pl.ds(2 * heads * block, ID_ROWS), :] = tag.astype(jnp.float32).astype(out_ref.dtype)
    for which, ref in enumerate((k_ref, v_ref)):
        scratch[which] = ref[...].astype(jnp.float32)
    for which in range(2):
        for g in range(heads):
            out_ref[pl.ds((which * heads + g) * block, block), :] = scratch[
                which, pl.ds(g, block, stride=heads), :
            ].astype(out_ref.dtype)


def local_kernel(
    len_ref, q_ref, nk_ref, nv_ref, sk_ref, sv_ref, acc_ref, top_ref, sum_ref,
    q_buf, nk_buf, nv_buf, sk_buf, sv_buf, kf, vf, sems, *, first, count, heads, steps, group, scale,
):
    slots = sk_ref.shape[1] // heads
    rows = steps * group

    def copies(i):
        r = first + i
        return [
            pltpu.make_async_copy(a.at[r], b.at[i], sems.at[i, j])
            for j, (a, b) in enumerate(
                ((q_ref, q_buf), (nk_ref, nk_buf), (nv_ref, nv_buf), (sk_ref, sk_buf), (sv_ref, sv_buf))
            )
        ]

    for i in range(count):
        for c in copies(i):
            c.start()
    key_slot = lax.broadcasted_iota(jnp.int32, (rows, slots), 1)
    fresh_col = lax.broadcasted_iota(jnp.int32, (rows, steps * heads), 1)
    fresh_row = lax.broadcasted_iota(jnp.int32, (rows, steps * heads), 0)
    fresh_seen = fresh_col // heads <= fresh_row // group
    factor = scale * math.log2(math.e)
    for i in range(count):
        for c in copies(i):
            c.wait()
        shown = key_slot < len_ref[first + i]
        kf[i % 2] = sk_buf[i].astype(jnp.float32)
        vf[i % 2] = sv_buf[i].astype(jnp.float32)
        fresh_k, fresh_v = nk_buf[i], nv_buf[i]
        for g in range(heads):
            q = jnp.concatenate(
                [q_buf[i, s, g * group : (g + 1) * group, :] for s in range(steps)], axis=0
            )
            k = kf[i % 2, pl.ds(g, slots, stride=heads), :].astype(jnp.bfloat16)
            v = vf[i % 2, pl.ds(g, slots, stride=heads), :].astype(jnp.bfloat16)
            scores = lax.dot_general(q, k, NT, preferred_element_type=jnp.float32)
            scores = jnp.where(shown, scores, -jnp.inf)
            fresh = lax.dot_general(q, fresh_k, NT, preferred_element_type=jnp.float32)
            fresh = jnp.where(fresh_seen & (fresh_col % heads == g), fresh, -jnp.inf)
            top = jnp.maximum(
                jnp.max(scores, axis=1, keepdims=True), jnp.max(fresh, axis=1, keepdims=True)
            )
            w = jnp.exp2((scores - top) * factor)
            wf = jnp.exp2((fresh - top) * factor)
            total = jnp.sum(w, axis=1, keepdims=True) + jnp.sum(wf, axis=1, keepdims=True)
            acc_ref[i, g] = jnp.dot(
                w.astype(jnp.bfloat16), v, preferred_element_type=jnp.float32
            ) + jnp.dot(wf.astype(jnp.bfloat16), fresh_v, preferred_element_type=jnp.float32)
            top_ref[i, g] = jnp.broadcast_to(top, top_ref.shape[2:])
            sum_ref[i, g] = jnp.broadcast_to(total, sum_ref.shape[2:])


def prior_kernel(list_ref, q_ref, *refs, blocks, pieces, heads, block, named, steps, group, scale):
    parts = refs[: 3 * pieces]
    loads = refs[3 * pieces : 3 * pieces + blocks]
    out_ref, kv, slot_of, sems = refs[3 * pieces + blocks :]
    copies = [pltpu.make_async_copy(loads[p], kv.at[p], sems.at[p]) for p in range(blocks)]
    for c in copies:
        c.start()
    for c in copies:
        c.wait()
    for p in range(blocks):
        tag = kv[p, pl.ds(2 * heads * block, ID_ROWS), :].astype(jnp.float32)
        number = jnp.max(tag[: ID_ROWS // 2] * 256.0 + tag[ID_ROWS // 2 :]).astype(jnp.int32)
        slot_of[number] = p
    factor = scale * math.log2(math.e)
    requests = q_ref.shape[0]
    each = requests // pieces
    for r in range(requests):
        slots = [slot_of[list_ref[r, j]] for j in range(named)]
        acc_ref, top_ref, sum_ref = parts[3 * (r // each) : 3 * (r // each) + 3]
        i = r % each
        for g in range(heads):
            q = jnp.concatenate(
                [q_ref[r, s, g * group : (g + 1) * group, :] for s in range(steps)], axis=0
            )
            k = jnp.concatenate([kv[s, pl.ds(g * block, block), :] for s in slots], axis=0)
            v = jnp.concatenate([kv[s, pl.ds((heads + g) * block, block), :] for s in slots], axis=0)
            scores = lax.dot_general(q, k, NT, preferred_element_type=jnp.float32)
            local_top = top_ref[i, g][:, :1]
            top = jnp.maximum(local_top, jnp.max(scores, axis=1, keepdims=True))
            w = jnp.exp2((scores - top) * factor)
            keep = jnp.exp2((local_top - top) * factor)
            total = sum_ref[i, g][:, :1] * keep + jnp.sum(w, axis=1, keepdims=True)
            mixed = acc_ref[i, g] * keep + jnp.dot(
                w.astype(jnp.bfloat16), v, preferred_element_type=jnp.float32
            )
            mixed = (mixed / total).astype(out_ref.dtype)
            for s in range(steps):
                out_ref[r, s, g * group : (g + 1) * group, :] = mixed[s * group : (s + 1) * group]


def per_device(
    queries, new_keys, new_values, suffix_keys, suffix_values, suffix_len,
    prefix_keys, prefix_values, block_ids, block_lists, *, devices, pieces=4,
):
    requests, steps, head_count, width = queries.shape
    heads = new_keys.shape[2]
    group = head_count // heads
    slots = suffix_keys.shape[1]
    block = prefix_keys.shape[1]
    named = block_lists.shape[1]
    scale = 1.0 / math.sqrt(width)
    rows = steps * group
    any_space = pl.BlockSpec(memory_space=pl.ANY)
    vmem = pl.BlockSpec(memory_space=pltpu.VMEM)
    smem = pl.BlockSpec(memory_space=pltpu.SMEM)
    load_rows = 2 * heads * block + ID_ROWS

    load = pl.pallas_call(
        functools.partial(pack_kernel, heads=heads, block=block),
        out_shape=jax.ShapeDtypeStruct((load_rows, width), prefix_keys.dtype),
        in_specs=[smem, vmem, vmem],
        out_specs=vmem,
        scratch_shapes=[pltpu.VMEM((2, heads * block, width), jnp.float32)],
        name="pack",
    )(
        block_ids,
        prefix_keys.reshape(heads * block, width),
        prefix_values.reshape(heads * block, width),
    )

    chips = devices // 2
    ring = ring_of_chips(chips)
    ahead = [(2 * a + c, 2 * b + c) for a, b in zip(ring, ring[1:] + ring[:1]) for c in range(2)]
    back = [(b, a) for a, b in ahead]
    swap = [(d, d ^ 1) for d in range(devices)]
    loads = [load, lax.ppermute(load, "loop", swap)]
    right = left = load
    for step in range(chips // 2):
        right = lax.ppermute(right, "loop", ahead)
        loads += [right, lax.ppermute(right, "loop", swap)]
        if 2 * step + 2 < chips:
            left = lax.ppermute(left, "loop", back)
            loads += [left, lax.ppermute(left, "loop", swap)]

    each = requests // pieces
    flat_keys = suffix_keys.reshape(requests, slots * heads, width)
    flat_values = suffix_values.reshape(requests, slots * heads, width)
    fresh_keys = new_keys.reshape(requests, steps * heads, width)
    fresh_values = new_values.reshape(requests, steps * heads, width)
    parts = []
    stat = jax.ShapeDtypeStruct((each, heads, rows, width), jnp.float32)
    for piece in range(pieces):
        parts += pl.pallas_call(
            functools.partial(
                local_kernel, first=piece * each, count=each, heads=heads, steps=steps, group=group, scale=scale
            ),
            out_shape=[stat] * 3,
            in_specs=[smem] + [any_space] * 5,
            out_specs=[vmem] * 3,
            scratch_shapes=[
                pltpu.VMEM((each, steps, head_count, width), queries.dtype),
                pltpu.VMEM((each, steps * heads, width), queries.dtype),
                pltpu.VMEM((each, steps * heads, width), queries.dtype),
                pltpu.VMEM((each, slots * heads, width), queries.dtype),
                pltpu.VMEM((each, slots * heads, width), queries.dtype),
                pltpu.VMEM((2, slots * heads, width), jnp.float32),
                pltpu.VMEM((2, slots * heads, width), jnp.float32),
                pltpu.SemaphoreType.DMA((each, 5)),
            ],
            name=f"local{piece}",
        )(suffix_len, queries, fresh_keys, fresh_values, flat_keys, flat_values)

    return pl.pallas_call(
        functools.partial(
            prior_kernel, blocks=devices, pieces=pieces, heads=heads, block=block, named=named,
            steps=steps, group=group, scale=scale,
        ),
        out_shape=jax.ShapeDtypeStruct(queries.shape, queries.dtype),
        in_specs=[smem, vmem] + [vmem] * (3 * pieces) + [any_space] * devices,
        out_specs=vmem,
        scratch_shapes=[
            pltpu.VMEM((devices, load_rows, width), queries.dtype),
            pltpu.SMEM((devices,), jnp.int32),
            pltpu.SemaphoreType.DMA((devices,)),
        ],
        name="prior",
    )(block_lists, queries, *parts, *loads)


def solution(mesh):
    split = ("groups", "loop")
    in_specs = tuple(
        P(split, *([None] * (rank - 1))) for rank in (4, 4, 4, 4, 4, 1, 4, 4, 1, 2)
    )
    return jax.shard_map(
        functools.partial(per_device, devices=mesh.shape["loop"]),
        mesh=mesh, in_specs=in_specs, out_specs=P(split, None, None, None), check_vma=False,
    )
```

```python
import functools
import math

import jax
import jax.numpy as jnp
from jax import lax
from jax.experimental import pallas as pl
from jax.experimental.pallas import tpu as pltpu
from jax.sharding import PartitionSpec as P


ID_ROWS = 16
NT = (((1,), (1,)), ((), ()))


def ring_of_chips(chips):
    inner = 1 << ((chips.bit_length() - 1) // 2)
    outer = chips // inner
    if inner == 1 or outer % 2:
        return list(range(chips))
    walk = [(a, 0) for a in range(outer)]
    for step, a in enumerate(reversed(range(outer))):
        row = [(a, b) for b in range(1, inner)]
        walk += row if step % 2 == 0 else row[::-1]
    return [a * inner + b for a, b in walk]


def pack_kernel(id_ref, k_hbm, v_hbm, out_ref, raw, wide, sems, *, heads, block):
    copies = [pltpu.make_async_copy(a, raw.at[i], sems.at[i]) for i, a in enumerate((k_hbm, v_hbm))]
    for c in copies:
        c.start()
    number = id_ref[0]
    high, low = number // 256, number % 256
    row = lax.broadcasted_iota(jnp.int32, (ID_ROWS, out_ref.shape[1]), 0)
    tag = jnp.where(row < ID_ROWS // 2, high, low)
    out_ref[pl.ds(2 * heads * block, ID_ROWS), :] = tag.astype(jnp.float32).astype(out_ref.dtype)
    for i in range(2):
        copies[i].wait()
        wide[i] = raw[i].astype(jnp.float32)
        for g in range(heads):
            out_ref[pl.ds((i * heads + g) * block, block), :] = wide[
                i, pl.ds(g, block, stride=heads), :
            ].astype(out_ref.dtype)


def load_kernel(*refs, arrays):
    sources, targets, sems = refs[:arrays], refs[arrays : 2 * arrays], refs[2 * arrays]
    copies = [pltpu.make_async_copy(a, b, sems.at[i]) for i, (a, b) in enumerate(zip(sources, targets))]
    for c in copies:
        c.start()
    for c in copies:
        c.wait()


def local_kernel(
    len_ref, q_ref, nk_ref, nv_ref, sk_ref, sv_ref, out_ref, stat_ref, kf, vf,
    *, first, count, heads, steps, group, factor,
):
    slots = sk_ref.shape[1] // heads
    rows = steps * group
    fresh_col = lax.broadcasted_iota(jnp.int32, (rows, steps * heads), 1)
    fresh_row = lax.broadcasted_iota(jnp.int32, (rows, steps * heads), 0)
    fresh_seen = fresh_col // heads <= fresh_row // group
    fresh_bias = [
        jnp.where(fresh_seen & (fresh_col % heads == g), 0.0, -jnp.inf) for g in range(heads)
    ]
    slot = lax.broadcasted_iota(jnp.int32, (1, slots), 1)
    for i in range(count):
        r = first + i
        kf[i % 2] = sk_ref[r].astype(jnp.float32)
        vf[i % 2] = sv_ref[r].astype(jnp.float32)
        bias = jnp.where(slot < len_ref[r], 0.0, -jnp.inf)
        fresh_k, fresh_v = nk_ref[r], nv_ref[r]
        scores, fresh, values = [], [], []
        for g in range(heads):
            q = jnp.concatenate(
                [q_ref[r, s, g * group : (g + 1) * group, :] for s in range(steps)], axis=0
            )
            k = kf[i % 2, pl.ds(g, slots, stride=heads), :].astype(jnp.bfloat16)
            values.append(vf[i % 2, pl.ds(g, slots, stride=heads), :].astype(jnp.bfloat16))
            scores.append(lax.dot_general(q, k, NT, preferred_element_type=jnp.float32) + bias)
            fresh.append(
                lax.dot_general(q, fresh_k, NT, preferred_element_type=jnp.float32) + fresh_bias[g]
            )
        for g in range(heads):
            top = jnp.maximum(
                jnp.max(scores[g], axis=1, keepdims=True), jnp.max(fresh[g], axis=1, keepdims=True)
            )
            w = jnp.exp2((scores[g] - top) * factor)
            wf = jnp.exp2((fresh[g] - top) * factor)
            total = jnp.sum(w, axis=1, keepdims=True) + jnp.sum(wf, axis=1, keepdims=True)
            mixed = jnp.dot(
                w.astype(jnp.bfloat16), values[g], preferred_element_type=jnp.float32
            ) + jnp.dot(wf.astype(jnp.bfloat16), fresh_v, preferred_element_type=jnp.float32)
            out_ref[i, g] = mixed / total
            stat_ref[i, g] = jnp.broadcast_to(top * factor + jnp.log2(total), stat_ref.shape[2:])


def prior_kernel(
    list_ref, q_ref, *refs, blocks, spans, heads, block, named, steps, group, factor,
):
    pieces = len(spans)
    mixes, stats = refs[: 2 * pieces : 2], refs[1 : 2 * pieces : 2]
    loads = refs[2 * pieces : 2 * pieces + blocks]
    out_hbm, kv, out_ref, slot_of, sems = refs[2 * pieces + blocks :]
    home = [(piece, i) for piece, (_, count) in enumerate(spans) for i in range(count)]
    requests = q_ref.shape[0]
    half = ID_ROWS // 2
    outs = [pltpu.make_async_copy(out_ref.at[r], out_hbm.at[r], sems.at[r]) for r in range(requests)]
    for p in range(blocks):
        tag = loads[p][pl.ds(2 * heads * block, ID_ROWS), :].astype(jnp.float32)
        slot_of[jnp.max(tag[:half] * 256.0 + tag[half:]).astype(jnp.int32)] = p
    for p in range(blocks):
        kv[p] = loads[p][pl.ds(0, 2 * heads * block), :]
    for r in range(requests):
        places = [slot_of[list_ref[j, r]] for j in range(named)]
        mix_ref, stat_ref, i = mixes[home[r][0]], stats[home[r][0]], home[r][1]
        scores, values = [], []
        for g in range(heads):
            q = jnp.concatenate(
                [q_ref[r, s, g * group : (g + 1) * group, :] for s in range(steps)], axis=0
            )
            k = jnp.concatenate([kv[p, pl.ds(g * block, block), :] for p in places], axis=0)
            values.append(
                jnp.concatenate([kv[p, pl.ds((heads + g) * block, block), :] for p in places], axis=0)
            )
            scores.append(lax.dot_general(q, k, NT, preferred_element_type=jnp.float32))
        for g in range(heads):
            near = stat_ref[i, g]
            best = jnp.max(scores[g], axis=1, keepdims=True)
            own = jnp.broadcast_to(best, near.shape) * factor
            top = jnp.maximum(near, own)
            w = jnp.exp2((scores[g] - best) * factor)
            keep, add = jnp.exp2(near - top), jnp.exp2(own - top)
            total = keep + add * jnp.sum(w, axis=1, keepdims=True)
            mixed = mix_ref[i, g] * keep + add * jnp.dot(
                w.astype(jnp.bfloat16), values[g], preferred_element_type=jnp.float32
            )
            mixed = (mixed / total).astype(out_ref.dtype)
            for s in range(steps):
                out_ref[r, s, g * group : (g + 1) * group, :] = mixed[s * group : (s + 1) * group]
        outs[r].start()
    for c in outs:
        c.wait()


def per_device(
    queries, new_keys, new_values, suffix_keys, suffix_values, suffix_len,
    prefix_keys, prefix_values, block_ids, block_lists, *, devices, pieces=3,
):
    requests, steps, head_count, width = queries.shape
    heads = new_keys.shape[2]
    group = head_count // heads
    slots = suffix_keys.shape[1]
    block = prefix_keys.shape[1]
    named = block_lists.shape[1]
    factor = math.log2(math.e) / math.sqrt(width)
    rows = steps * group
    kind = queries.dtype
    far = pl.BlockSpec(memory_space=pltpu.HBM)
    vmem = pl.BlockSpec(memory_space=pltpu.VMEM)
    smem = pl.BlockSpec(memory_space=pltpu.SMEM)
    load_rows = 2 * heads * block + ID_ROWS
    tie = lambda *arrays: lax.optimization_barrier(arrays)
    away = functools.partial(pltpu.with_memory_space_constraint, memory_space=pltpu.HBM)
    near = functools.partial(pltpu.with_memory_space_constraint, memory_space=pltpu.VMEM)

    load = pl.pallas_call(
        functools.partial(pack_kernel, heads=heads, block=block),
        out_shape=pltpu.VMEM((load_rows, width), kind),
        in_specs=[smem, far, far],
        out_specs=vmem,
        scratch_shapes=[
            pltpu.VMEM((2, heads * block, width), kind),
            pltpu.VMEM((2, heads * block, width), jnp.float32),
            pltpu.SemaphoreType.DMA((2,)),
        ],
        compiler_params=pltpu.CompilerParams(vmem_limit_bytes=4 << 20),
        name="pack",
    )(
        block_ids,
        away(prefix_keys.reshape(heads * block, width)),
        away(prefix_values.reshape(heads * block, width)),
    )

    flat = [
        queries,
        new_keys.reshape(requests, steps * heads, width),
        new_values.reshape(requests, steps * heads, width),
        suffix_keys.reshape(requests, slots * heads, width),
        suffix_values.reshape(requests, slots * heads, width),
    ]

    def fetch(arrays):
        return pl.pallas_call(
            functools.partial(load_kernel, arrays=len(arrays)),
            out_shape=[pltpu.VMEM(x.shape, x.dtype) for x in arrays],
            in_specs=[far] * len(arrays),
            out_specs=[vmem] * len(arrays),
            scratch_shapes=[pltpu.SemaphoreType.DMA((len(arrays),))],
            compiler_params=pltpu.CompilerParams(vmem_limit_bytes=1 << 20),
            name="fetch",
        )(*[away(x) for x in arrays])

    def local(span, lengths, held):
        first, count = span
        return pl.pallas_call(
            functools.partial(
                local_kernel, first=first, count=count, heads=heads, steps=steps, group=group, factor=factor
            ),
            out_shape=[pltpu.VMEM((count, heads, rows, width), jnp.float32)] * 2,
            in_specs=[smem] + [vmem] * 5,
            out_specs=[vmem] * 2,
            scratch_shapes=[pltpu.VMEM((2, slots * heads, width), jnp.float32)] * 2,
            compiler_params=pltpu.CompilerParams(vmem_limit_bytes=8 << 20),
            name=f"local{first}",
        )(lengths, *[near(x) for x in held])

    sizes = [(requests + p) // pieces for p in range(pieces)][::-1]
    spans = [(sum(sizes[:p]), sizes[p]) for p in range(pieces)]
    chips = devices // 2
    ring = ring_of_chips(chips)
    ahead = [(2 * a + c, 2 * b + c) for a, b in zip(ring, ring[1:] + ring[:1]) for c in range(2)]
    back = [(b, a) for a, b in ahead]
    swap = [(d, d ^ 1) for d in range(devices)]
    loads = [load, lax.ppermute(load, "loop", swap)]
    right = left = load
    held, parts, fresh = [], [], []
    rounds = chips // 2
    for step in range(rounds):
        if step == 0:
            right, *flat = tie(load, *flat)
            left = right
            held = fresh = fetch(flat)
        else:
            right, *fresh = tie(right, *fresh)
            lengths, left = tie(suffix_len, left)
            if step == 1:
                held, fresh = fresh, []
            parts += fresh
            fresh = local(spans[step - 1], lengths, held) if step <= pieces else []
        nearer = lax.ppermute(right, "loop", ahead)
        farther = lax.ppermute(left, "loop", back) if 2 * step + 2 < chips else left
        right = nearer
        if step == rounds - 1:
            right, *fresh = tie(right, *fresh)
        loads += [right, lax.ppermute(right, "loop", swap)]
        if 2 * step + 2 < chips:
            left = farther
            loads += [left, lax.ppermute(left, "loop", swap)]
    parts += fresh
    for piece in range(len(parts) // 2, pieces):
        parts += local(spans[piece], suffix_len, held)

    return pl.pallas_call(
        functools.partial(
            prior_kernel, blocks=devices, spans=spans, heads=heads, block=block, named=named,
            steps=steps, group=group, factor=factor,
        ),
        out_shape=jax.ShapeDtypeStruct(queries.shape, kind),
        in_specs=[smem] + [vmem] * (1 + 2 * pieces + devices),
        out_specs=far,
        scratch_shapes=[
            pltpu.VMEM((devices, 2 * heads * block, width), kind),
            pltpu.VMEM(queries.shape, kind),
            pltpu.SMEM((devices,), jnp.int32),
            pltpu.SemaphoreType.DMA((requests,)),
        ],
        compiler_params=pltpu.CompilerParams(vmem_limit_bytes=24 << 20),
        name="prior",
    )(block_lists.T, near(held[0]), *[near(x) for x in parts], *[near(x) for x in loads])


def solution(mesh):
    split = ("groups", "loop")
    in_specs = tuple(
        P(split, *([None] * (rank - 1))) for rank in (4, 4, 4, 4, 4, 1, 4, 4, 1, 2)
    )
    return jax.shard_map(
        functools.partial(per_device, devices=mesh.shape["loop"]),
        mesh=mesh, in_specs=in_specs, out_specs=P(split, None, None, None), check_vma=False,
    )
```

```python
import functools
import math

import jax
import jax.numpy as jnp
from jax import lax
from jax.experimental import pallas as pl
from jax.experimental.pallas import tpu as pltpu
from jax.sharding import PartitionSpec as P


ID_ROWS = 16
NT = (((1,), (1,)), ((), ()))


def ring_of_chips(chips):
    inner = 1 << ((chips.bit_length() - 1) // 2)
    outer = chips // inner
    if inner == 1 or outer % 2:
        return list(range(chips))
    walk = [(a, 0) for a in range(outer)]
    for step, a in enumerate(reversed(range(outer))):
        row = [(a, b) for b in range(1, inner)]
        walk += row if step % 2 == 0 else row[::-1]
    return [a * inner + b for a, b in walk]


def pack_kernel(id_ref, k_hbm, v_hbm, out_ref, raw, wide, sems, *, heads, block):
    copies = [pltpu.make_async_copy(a, raw.at[i], sems.at[i]) for i, a in enumerate((k_hbm, v_hbm))]
    for c in copies:
        c.start()
    number = id_ref[0]
    high, low = number // 256, number % 256
    row = lax.broadcasted_iota(jnp.int32, (ID_ROWS, out_ref.shape[1]), 0)
    tag = jnp.where(row < ID_ROWS // 2, high, low)
    out_ref[pl.ds(2 * heads * block, ID_ROWS), :] = tag.astype(jnp.float32).astype(out_ref.dtype)
    for i in range(2):
        copies[i].wait()
        wide[i] = raw[i].astype(jnp.float32)
        for g in range(heads):
            out_ref[pl.ds((i * heads + g) * block, block), :] = wide[
                i, pl.ds(g, block, stride=heads), :
            ].astype(out_ref.dtype)


def local_kernel(len_ref, *refs, first, count, fetch, heads, steps, group, factor):
    if fetch:
        sources, refs, (lengths_ref, len_sem, sems) = refs[:5], refs[5:-3], refs[-3:]
        len_copy = pltpu.make_async_copy(len_ref, lengths_ref, len_sem)
        len_copy.start()
        len_ref = lengths_ref
        copies = [
            [
                pltpu.make_async_copy(a.at[r], b.at[r], sems.at[r, j])
                for j, (a, b) in enumerate(zip(sources, refs[:5]))
            ]
            for r in range(sources[0].shape[0])
        ]
        for c in sum(copies, []):
            c.start()
        len_copy.wait()
    q_ref, nk_ref, nv_ref, sk_ref, sv_ref, out_ref, top_ref, sum_ref, kf, vf = refs
    slots = sk_ref.shape[1] // heads
    rows = steps * group
    fresh_col = lax.broadcasted_iota(jnp.int32, (rows, steps * heads), 1)
    fresh_row = lax.broadcasted_iota(jnp.int32, (rows, steps * heads), 0)
    fresh_seen = fresh_col // heads <= fresh_row // group
    fresh_bias = [
        jnp.where(fresh_seen & (fresh_col % heads == g), 0.0, -jnp.inf) for g in range(heads)
    ]
    slot = lax.broadcasted_iota(jnp.int32, (1, slots), 1)
    for i in range(count):
        r = first + i
        if fetch:
            for c in copies[r]:
                c.wait()
        kf[i % 2] = sk_ref[r].astype(jnp.float32)
        vf[i % 2] = sv_ref[r].astype(jnp.float32)
        bias = jnp.where(slot < len_ref[r], 0.0, -jnp.inf)
        fresh_k, fresh_v = nk_ref[r], nv_ref[r]
        scores, fresh, values = [], [], []
        for g in range(heads):
            q = jnp.concatenate(
                [q_ref[r, s, g * group : (g + 1) * group, :] for s in range(steps)], axis=0
            )
            k = kf[i % 2, pl.ds(g, slots, stride=heads), :].astype(jnp.bfloat16)
            values.append(vf[i % 2, pl.ds(g, slots, stride=heads), :].astype(jnp.bfloat16))
            scores.append(lax.dot_general(q, k, NT, preferred_element_type=jnp.float32) + bias)
            fresh.append(
                lax.dot_general(q, fresh_k, NT, preferred_element_type=jnp.float32) + fresh_bias[g]
            )
        for g in range(heads):
            top = jnp.maximum(
                jnp.max(scores[g], axis=1, keepdims=True), jnp.max(fresh[g], axis=1, keepdims=True)
            )
            w = jnp.exp2((scores[g] - top) * factor)
            wf = jnp.exp2((fresh[g] - top) * factor)
            total = jnp.sum(w, axis=1, keepdims=True) + jnp.sum(wf, axis=1, keepdims=True)
            out_ref[i, g] = jnp.dot(
                w.astype(jnp.bfloat16), values[g], preferred_element_type=jnp.float32
            ) + jnp.dot(wf.astype(jnp.bfloat16), fresh_v, preferred_element_type=jnp.float32)
            top_ref[i, g] = jnp.broadcast_to(top, top_ref.shape[2:])
            sum_ref[i, g] = jnp.broadcast_to(total, sum_ref.shape[2:])
    if fetch:
        for c in sum(copies[first + count :], []):
            c.wait()


def prior_kernel(
    list_ref, q_ref, *refs, blocks, layout, spans, heads, block, named, steps, group, factor,
):
    pieces = len(spans)
    parts, loads = refs[: 3 * pieces], refs[3 * pieces : 3 * pieces + len(layout)]
    out_hbm, kv, out_ref, slot_of, sems, gather_sem = refs[3 * pieces + len(layout) :]
    home = [(parts[3 * p : 3 * p + 3], i) for p, (_, count) in enumerate(spans) for i in range(count)]
    requests, lanes = q_ref.shape[0], q_ref.shape[3]
    half = ID_ROWS // 2
    outs = [pltpu.make_async_copy(out_ref.at[r], out_hbm.at[r], sems.at[r]) for r in range(requests)]
    for ref, place in zip(loads, layout):
        if place is None:
            whole = pltpu.make_async_copy(ref, kv, gather_sem)
            whole.start()
            whole.wait()
        else:
            kv[place[0], pl.ds(place[1], ref.shape[0]), :] = ref[...]
    for p in range(blocks):
        tag = kv[p, pl.ds(2 * heads * block, ID_ROWS), :].astype(jnp.float32)
        slot_of[jnp.max(tag[:half] * 256.0 + tag[half:]).astype(jnp.int32)] = p
    for r in range(requests):
        places = [slot_of[list_ref[j, r]] for j in range(named)]
        (near_out, near_top, near_sum), i = home[r]
        scores, values = [], []
        for g in range(heads):
            q = jnp.concatenate(
                [q_ref[r, s, g * group : (g + 1) * group, :] for s in range(steps)], axis=0
            )
            k = jnp.concatenate([kv[p, pl.ds(g * block, block), :] for p in places], axis=0)
            values.append(
                jnp.concatenate([kv[p, pl.ds((heads + g) * block, block), :] for p in places], axis=0)
            )
            scores.append(lax.dot_general(q, k, NT, preferred_element_type=jnp.float32))
        for g in range(heads):
            near = near_top[i, g]
            best = jnp.max(scores[g], axis=1, keepdims=True)
            top = jnp.maximum(near, jnp.broadcast_to(best, near.shape))
            w = [
                jnp.exp2((scores[g][:, c : c + lanes] - top) * factor)
                for c in range(0, named * block, lanes)
            ]
            keep = jnp.exp2((near - top) * factor)
            total = near_sum[i, g] * keep + jnp.sum(sum(w[1:], w[0]), axis=1, keepdims=True)
            weights = jnp.concatenate([x.astype(jnp.bfloat16) for x in w], axis=1)
            mixed = near_out[i, g] * keep + jnp.dot(
                weights, values[g], preferred_element_type=jnp.float32
            )
            mixed = (mixed / total).astype(out_ref.dtype)
            for s in range(steps):
                out_ref[r, s, g * group : (g + 1) * group, :] = mixed[s * group : (s + 1) * group]
        outs[r].start()
    for c in outs:
        c.wait()


def partial_kernel(
    list_ref, q_ref, *refs, have, spans, collect, heads, block, named, steps, group, factor,
):
    pieces = len(spans)
    parts, refs = refs[: 3 * pieces], refs[3 * pieces :]
    home = [(parts[3 * p : 3 * p + 3], i) for p, (_, count) in enumerate(spans) for i in range(count)]
    if collect:
        loads, (kv, out_ref, top_ref, sum_ref, slot_of) = refs[:have], refs[have:]
        for p in range(have):
            kv[p] = loads[p][...]
    else:
        kv, out_ref, top_ref, sum_ref, slot_of = refs
    lanes = q_ref.shape[3]
    half = ID_ROWS // 2
    for p in range(slot_of.shape[0]):
        slot_of[p] = -1
    for p in range(have):
        tag = kv[p, pl.ds(2 * heads * block, ID_ROWS), :].astype(jnp.float32)
        slot_of[jnp.max(tag[:half] * 256.0 + tag[half:]).astype(jnp.int32)] = p
    which = lax.broadcasted_iota(jnp.int32, (1, named * block), 1) // block
    for o, ((near_out, near_top, near_sum), i) in enumerate(home):
        r = spans[0][0] + o
        spots = [slot_of[list_ref[j, r]] for j in range(named)]
        places = [jnp.maximum(x, 0) for x in spots]
        bias = jnp.zeros(which.shape, jnp.float32)
        for j in range(named):
            bias = jnp.where(which == j, jnp.where(spots[j] < 0, -jnp.inf, 0.0), bias)
        scores, values = [], []
        for g in range(heads):
            q = jnp.concatenate(
                [q_ref[r, s, g * group : (g + 1) * group, :] for s in range(steps)], axis=0
            )
            k = jnp.concatenate([kv[p, pl.ds(g * block, block), :] for p in places], axis=0)
            values.append(
                jnp.concatenate([kv[p, pl.ds((heads + g) * block, block), :] for p in places], axis=0)
            )
            scores.append(lax.dot_general(q, k, NT, preferred_element_type=jnp.float32) + bias)
        for g in range(heads):
            near = near_top[i, g]
            best = jnp.max(scores[g], axis=1, keepdims=True)
            top = jnp.maximum(near, jnp.broadcast_to(best, near.shape))
            w = [
                jnp.exp2((scores[g][:, c : c + lanes] - top) * factor)
                for c in range(0, named * block, lanes)
            ]
            keep = jnp.exp2((near - top) * factor)
            sum_ref[o, g] = near_sum[i, g] * keep + jnp.sum(sum(w[1:], w[0]), axis=1, keepdims=True)
            weights = jnp.concatenate([x.astype(jnp.bfloat16) for x in w], axis=1)
            out_ref[o, g] = near_out[i, g] * keep + jnp.dot(
                weights, values[g], preferred_element_type=jnp.float32
            )
            top_ref[o, g] = top


def final_kernel(list_ref, q_ref, *refs, spans, batch, heads, block, named, steps, group, factor):
    pieces = len(spans)
    parts, (one_ref, two_ref, out_hbm, out_ref, sems) = refs[: 3 * pieces], refs[3 * pieces :]
    home = [(parts[3 * p : 3 * p + 3], i) for p, (_, count) in enumerate(spans) for i in range(count)]
    half, rows = ID_ROWS // 2, steps * group
    loads = (one_ref, two_ref)
    numbers = []
    for load in loads:
        tag = load[pl.ds(2 * heads * block, ID_ROWS), :].astype(jnp.float32)
        numbers.append(jnp.max(tag[:half] * 256.0 + tag[half:]).astype(jnp.int32))
    which = lax.broadcasted_iota(jnp.int32, (1, 2 * block), 1) // block
    outs = []
    for start in range(0, len(home), batch):
        span = range(start, min(start + batch, len(home)))
        biases = []
        for r in span:
            bias = jnp.full(which.shape, -jnp.inf, jnp.float32)
            for b in range(2):
                asked = list_ref[0, r] == numbers[b]
                for j in range(1, named):
                    asked = jnp.logical_or(asked, list_ref[j, r] == numbers[b])
                bias = jnp.where(which == b, jnp.where(asked, 0.0, -jnp.inf), bias)
            biases.append(bias)
        for g in range(heads):
            k = jnp.concatenate([x[pl.ds(g * block, block), :] for x in loads], axis=0)
            v = jnp.concatenate([x[pl.ds((heads + g) * block, block), :] for x in loads], axis=0)
            q = jnp.concatenate(
                [q_ref[r, s, g * group : (g + 1) * group, :] for r in span for s in range(steps)], axis=0
            )
            scores = lax.dot_general(q, k, NT, preferred_element_type=jnp.float32)
            weights, keeps, totals = [], [], []
            for o, r in enumerate(span):
                (_, near_top, near_sum), i = home[r]
                near = near_top[i, g]
                own = scores[o * rows : (o + 1) * rows] + biases[o]
                best = jnp.max(own, axis=1, keepdims=True)
                top = jnp.maximum(near, jnp.broadcast_to(best, near.shape))
                w = jnp.exp2((own - top[:, :1] if top.shape[1] != own.shape[1] else own - top) * factor)
                keep = jnp.exp2((near - top) * factor)
                totals.append(near_sum[i, g] * keep + jnp.sum(w, axis=1, keepdims=True))
                weights.append(w.astype(jnp.bfloat16))
                keeps.append(keep)
            mixed = jnp.dot(jnp.concatenate(weights, axis=0), v, preferred_element_type=jnp.float32)
            for o, r in enumerate(span):
                (near_out, _, _), i = home[r]
                out = near_out[i, g] * keeps[o] + mixed[o * rows : (o + 1) * rows]
                out = (out / totals[o]).astype(out_ref.dtype)
                for s in range(steps):
                    out_ref[r, s, g * group : (g + 1) * group, :] = out[s * group : (s + 1) * group]
        for r in span:
            outs.append(pltpu.make_async_copy(out_ref.at[r], out_hbm.at[r], sems.at[r]))
            outs[-1].start()
    for c in outs:
        c.wait()


def per_device(
    queries, new_keys, new_values, suffix_keys, suffix_values, suffix_len,
    prefix_keys, prefix_values, block_ids, block_lists, *, devices, pieces=3,
):
    requests, steps, head_count, width = queries.shape
    heads = new_keys.shape[2]
    group = head_count // heads
    slots = suffix_keys.shape[1]
    block = prefix_keys.shape[1]
    named = block_lists.shape[1]
    factor = math.log2(math.e) / math.sqrt(width)
    rows = steps * group
    kind = queries.dtype
    far = pl.BlockSpec(memory_space=pltpu.HBM)
    vmem = pl.BlockSpec(memory_space=pltpu.VMEM)
    smem = pl.BlockSpec(memory_space=pltpu.SMEM)
    load_rows = 2 * heads * block + ID_ROWS
    tie = lambda *arrays: lax.optimization_barrier(arrays)
    away = functools.partial(pltpu.with_memory_space_constraint, memory_space=pltpu.HBM)
    near = functools.partial(pltpu.with_memory_space_constraint, memory_space=pltpu.VMEM)
    limit = lambda mib: pltpu.CompilerParams(vmem_limit_bytes=mib << 20)

    load = pl.pallas_call(
        functools.partial(pack_kernel, heads=heads, block=block),
        out_shape=pltpu.VMEM((load_rows, width), kind),
        in_specs=[smem, far, far],
        out_specs=vmem,
        scratch_shapes=[
            pltpu.VMEM((2, heads * block, width), kind),
            pltpu.VMEM((2, heads * block, width), jnp.float32),
            pltpu.SemaphoreType.DMA((2,)),
        ],
        compiler_params=limit(4),
        name="pack",
    )(
        block_ids,
        away(prefix_keys.reshape(heads * block, width)),
        away(prefix_values.reshape(heads * block, width)),
    )

    flat = [
        queries,
        new_keys.reshape(requests, steps * heads, width),
        new_values.reshape(requests, steps * heads, width),
        suffix_keys.reshape(requests, slots * heads, width),
        suffix_values.reshape(requests, slots * heads, width),
    ]
    sizes = [(requests + p) // pieces for p in range(pieces)][::-1]
    spans = [(sum(sizes[:p]), sizes[p]) for p in range(pieces)]

    def local(piece, lengths, arrays):
        first, count = spans[piece]
        fetch = piece == 0
        stats = [pltpu.VMEM((count, heads, rows, width), jnp.float32)] * 3
        handed = [pltpu.VMEM(x.shape, x.dtype) for x in arrays] if fetch else []
        return pl.pallas_call(
            functools.partial(
                local_kernel, first=first, count=count, fetch=fetch, heads=heads, steps=steps,
                group=group, factor=factor,
            ),
            out_shape=handed + stats,
            in_specs=[far] * 6 if fetch else [smem] + [vmem] * 5,
            out_specs=[vmem] * len(handed + stats),
            scratch_shapes=[pltpu.VMEM((2, slots * heads, width), jnp.float32)] * 2
            + [
                pltpu.SMEM((requests,), jnp.int32),
                pltpu.SemaphoreType.DMA,
                pltpu.SemaphoreType.DMA((requests, 5)),
            ][: 3 * fetch],
            compiler_params=limit(8),
        )(away(lengths) if fetch else lengths, *[(away if fetch else near)(x) for x in arrays])

    chips = devices // 2
    rounds = chips // 2
    if 2 <= chips <= 16 and chips % 2 == 0:
        ring = ring_of_chips(chips)
        ahead = [(2 * a + c, 2 * b + c) for a, b in zip(ring, ring[1:] + ring[:1]) for c in range(2)]
        back = [(b, a) for a, b in ahead]
        swap = [(d, d ^ 1) for d in range(devices)]
        send = lambda x, pairs: lax.ppermute(x, "loop", pairs)
        right = left = load
        loads, layout, held, parts, fresh = [load], [(0, 0)], [], [], []
        waiting = [load]

        for step in range(rounds):
            if step == 0:
                right, *flat = tie(load, *flat)
                left, lengths = right, suffix_len
            else:
                right, *fresh = tie(right, *fresh)
                lengths, left = tie(suffix_len, left)
                if step == 1:
                    held, fresh = fresh[:5], fresh[5:]
                parts += fresh
                fresh = []
            last = step == rounds - 1
            ahead_of = send(right, ahead)
            back_of = left if last else send(left, back)
            if step < pieces:
                fresh = local(step, lengths, held or flat)
            if last:
                for x in waiting:
                    layout.append((len(layout), 0))
                    loads.append(send(x, swap))
            right, left = ahead_of, back_of
            if not last:
                for x in (right, left):
                    layout.append((len(layout), 0))
                    loads.append(x)
                    waiting.append(x)
        if rounds == 1:
            held, fresh = fresh[:5], fresh[5:]
        parts += fresh
        lists = block_lists.T
        for piece in range(min(rounds, pieces), pieces):
            parts += local(piece, suffix_len, held)
        sizes = dict(heads=heads, block=block, named=named, steps=steps, group=group, factor=factor)

        def partial(spans, parts, lists, sources, collect):
            count = sum(n for _, n in spans)
            have = devices - 2
            stats = [pltpu.VMEM((count, heads, rows, width), jnp.float32)] * 3
            made = [pltpu.VMEM((have, load_rows, width), kind)] if collect else []
            return pl.pallas_call(
                functools.partial(partial_kernel, have=have, spans=spans, collect=collect, **sizes),
                out_shape=made + stats,
                in_specs=[smem] + [vmem] * (1 + len(parts) + len(sources)),
                out_specs=[vmem] * len(made + stats),
                scratch_shapes=[pltpu.SMEM((devices,), jnp.int32)],
                compiler_params=limit(4),
            )(lists, *[near(x) for x in (held[0], *parts, *sources)])

        collected, *early = partial(spans[:1], parts[:3], lists, loads, True)
        right, *early = tie(right, *early)
        lists, right = tie(lists, right)
        other = send(right, swap)
        late = partial(spans[1:], parts[3:], lists, [collected], False)
        groups = [spans[0], (spans[1][0], requests - spans[1][0])]
        return pl.pallas_call(
            functools.partial(final_kernel, spans=groups, batch=-(-requests // 2), **sizes),
            out_shape=jax.ShapeDtypeStruct(queries.shape, kind),
            in_specs=[smem] + [vmem] * 9,
            out_specs=far,
            scratch_shapes=[pltpu.VMEM(queries.shape, kind), pltpu.SemaphoreType.DMA((requests,))],
            compiler_params=limit(8),
            name="final",
        )(lists, *[near(x) for x in (held[0], *early, *late, right, other)])
    gathered = lax.all_gather(load, "loop", axis=0)
    *held, a, b, c = local(0, suffix_len, flat)
    parts = [a, b, c]
    loads, layout = [away(gathered)], [None]
    for piece in range(1, pieces):
        parts += local(piece, suffix_len, held)

    return pl.pallas_call(
        functools.partial(
            prior_kernel, blocks=devices, layout=layout, spans=spans, heads=heads, block=block, named=named,
            steps=steps, group=group, factor=factor,
        ),
        out_shape=jax.ShapeDtypeStruct(queries.shape, kind),
        in_specs=[smem] + [vmem] * (1 + 3 * pieces) + [far if x is None else vmem for x in layout],
        out_specs=far,
        scratch_shapes=[
            pltpu.VMEM((devices, load_rows, width), kind),
            pltpu.VMEM(queries.shape, kind),
            pltpu.SMEM((devices,), jnp.int32),
            pltpu.SemaphoreType.DMA((requests,)),
            pltpu.SemaphoreType.DMA,
        ],
        compiler_params=limit(24),
        name="prior",
    )(block_lists.T, near(held[0]), *[near(x) for x in parts], *loads)


def solution(mesh):
    split = ("groups", "loop")
    in_specs = tuple(
        P(split, *([None] * (rank - 1))) for rank in (4, 4, 4, 4, 4, 1, 4, 4, 1, 2)
    )

    def body(*arrays):
        return per_device(*arrays, devices=mesh.shape["loop"])

    return jax.shard_map(
        body, mesh=mesh, in_specs=in_specs, out_specs=P(split, None, None, None), check_vma=False
    )
```

```python
import functools
import math

import jax
import jax.numpy as jnp
from jax import lax
from jax.experimental import pallas as pl
from jax.experimental.pallas import tpu as pltpu
from jax.sharding import PartitionSpec as P


ID_ROWS = 16
NT = (((1,), (1,)), ((), ()))


def ring_of_chips(chips):
    inner = 1 << ((chips.bit_length() - 1) // 2)
    outer = chips // inner
    if inner == 1 or outer % 2:
        return list(range(chips))
    walk = [(a, 0) for a in range(outer)]
    for step, a in enumerate(reversed(range(outer))):
        row = [(a, b) for b in range(1, inner)]
        walk += row if step % 2 == 0 else row[::-1]
    return [a * inner + b for a, b in walk]


def pack_kernel(id_ref, k_hbm, v_hbm, out_ref, raw, wide, sems, *, heads, block):
    copies = [pltpu.make_async_copy(a, raw.at[i], sems.at[i]) for i, a in enumerate((k_hbm, v_hbm))]
    for c in copies:
        c.start()
    number = id_ref[0]
    high, low = number // 256, number % 256
    row = lax.broadcasted_iota(jnp.int32, (ID_ROWS, out_ref.shape[1]), 0)
    tag = jnp.where(row < ID_ROWS // 2, high, low)
    out_ref[pl.ds(2 * heads * block, ID_ROWS), :] = tag.astype(jnp.float32).astype(out_ref.dtype)
    for i in range(2):
        copies[i].wait()
        wide[i] = raw[i].astype(jnp.float32)
        for g in range(heads):
            out_ref[pl.ds((i * heads + g) * block, block), :] = wide[
                i, pl.ds(g, block, stride=heads), :
            ].astype(out_ref.dtype)


def local_kernel(len_ref, *refs, first, count, fetch, heads, steps, group, factor):
    if fetch:
        sources, refs, (lengths_ref, len_sem, sems) = refs[:5], refs[5:-3], refs[-3:]
        len_copy = pltpu.make_async_copy(len_ref, lengths_ref, len_sem)
        len_copy.start()
        len_ref = lengths_ref
        copies = [
            [
                pltpu.make_async_copy(a.at[r], b.at[r], sems.at[r, j])
                for j, (a, b) in enumerate(zip(sources, refs[:5]))
            ]
            for r in range(sources[0].shape[0])
        ]
        for c in sum(copies, []):
            c.start()
        len_copy.wait()
    q_ref, nk_ref, nv_ref, sk_ref, sv_ref, out_ref, top_ref, sum_ref, kf, vf = refs
    slots = sk_ref.shape[1] // heads
    rows = steps * group
    fresh_col = lax.broadcasted_iota(jnp.int32, (rows, steps * heads), 1)
    fresh_row = lax.broadcasted_iota(jnp.int32, (rows, steps * heads), 0)
    fresh_seen = fresh_col // heads <= fresh_row // group
    fresh_bias = [
        jnp.where(fresh_seen & (fresh_col % heads == g), 0.0, -jnp.inf) for g in range(heads)
    ]
    slot = lax.broadcasted_iota(jnp.int32, (1, slots), 1)
    for i in range(count):
        r = first + i
        if fetch:
            for c in copies[r]:
                c.wait()
        kf[i % 2] = sk_ref[r].astype(jnp.float32)
        vf[i % 2] = sv_ref[r].astype(jnp.float32)
        bias = jnp.where(slot < len_ref[r], 0.0, -jnp.inf)
        fresh_k, fresh_v = nk_ref[r], nv_ref[r]
        scores, fresh, values = [], [], []
        for g in range(heads):
            q = jnp.concatenate(
                [q_ref[r, s, g * group : (g + 1) * group, :] for s in range(steps)], axis=0
            )
            k = kf[i % 2, pl.ds(g, slots, stride=heads), :].astype(jnp.bfloat16)
            values.append(vf[i % 2, pl.ds(g, slots, stride=heads), :].astype(jnp.bfloat16))
            scores.append(lax.dot_general(q, k, NT, preferred_element_type=jnp.float32) + bias)
            fresh.append(
                lax.dot_general(q, fresh_k, NT, preferred_element_type=jnp.float32) + fresh_bias[g]
            )
        for g in range(heads):
            top = jnp.maximum(
                jnp.max(scores[g], axis=1, keepdims=True), jnp.max(fresh[g], axis=1, keepdims=True)
            )
            w = jnp.exp2((scores[g] - top) * factor)
            wf = jnp.exp2((fresh[g] - top) * factor)
            total = jnp.sum(w, axis=1, keepdims=True) + jnp.sum(wf, axis=1, keepdims=True)
            out_ref[i, g] = jnp.dot(
                w.astype(jnp.bfloat16), values[g], preferred_element_type=jnp.float32
            ) + jnp.dot(wf.astype(jnp.bfloat16), fresh_v, preferred_element_type=jnp.float32)
            top_ref[i, g] = jnp.broadcast_to(top, top_ref.shape[2:])
            sum_ref[i, g] = jnp.broadcast_to(total, sum_ref.shape[2:])
    if fetch:
        for c in sum(copies[first + count :], []):
            c.wait()


def prior_kernel(
    list_ref, q_ref, *refs, blocks, layout, spans, heads, block, named, steps, group, factor,
):
    pieces = len(spans)
    parts, loads = refs[: 3 * pieces], refs[3 * pieces : 3 * pieces + len(layout)]
    out_hbm, kv, out_ref, slot_of, sems, gather_sem = refs[3 * pieces + len(layout) :]
    home = [(parts[3 * p : 3 * p + 3], i) for p, (_, count) in enumerate(spans) for i in range(count)]
    requests, lanes = q_ref.shape[0], q_ref.shape[3]
    half = ID_ROWS // 2
    outs = [pltpu.make_async_copy(out_ref.at[r], out_hbm.at[r], sems.at[r]) for r in range(requests)]
    for ref, place in zip(loads, layout):
        if place is None:
            whole = pltpu.make_async_copy(ref, kv, gather_sem)
            whole.start()
            whole.wait()
        else:
            kv[place[0], pl.ds(place[1], ref.shape[0]), :] = ref[...]
    for p in range(blocks):
        tag = kv[p, pl.ds(2 * heads * block, ID_ROWS), :].astype(jnp.float32)
        slot_of[(tag[:half] * 256.0 + tag[half:]).astype(jnp.int32)[0, 0]] = p
    for r in range(requests):
        places = [slot_of[list_ref[j, r]] for j in range(named)]
        (near_out, near_top, near_sum), i = home[r]
        scores, values = [], []
        for g in range(heads):
            q = jnp.concatenate(
                [q_ref[r, s, g * group : (g + 1) * group, :] for s in range(steps)], axis=0
            )
            k = jnp.concatenate([kv[p, pl.ds(g * block, block), :] for p in places], axis=0)
            values.append(
                jnp.concatenate([kv[p, pl.ds((heads + g) * block, block), :] for p in places], axis=0)
            )
            scores.append(lax.dot_general(q, k, NT, preferred_element_type=jnp.float32))
        for g in range(heads):
            near = near_top[i, g]
            best = jnp.max(scores[g], axis=1, keepdims=True)
            top = jnp.maximum(near, jnp.broadcast_to(best, near.shape))
            w = [
                jnp.exp2((scores[g][:, c : c + lanes] - top) * factor)
                for c in range(0, named * block, lanes)
            ]
            keep = jnp.exp2((near - top) * factor)
            total = near_sum[i, g] * keep + jnp.sum(sum(w[1:], w[0]), axis=1, keepdims=True)
            weights = jnp.concatenate([x.astype(jnp.bfloat16) for x in w], axis=1)
            mixed = near_out[i, g] * keep + jnp.dot(
                weights, values[g], preferred_element_type=jnp.float32
            )
            mixed = (mixed / total).astype(out_ref.dtype)
            for s in range(steps):
                out_ref[r, s, g * group : (g + 1) * group, :] = mixed[s * group : (s + 1) * group]
        outs[r].start()
    for c in outs:
        c.wait()


def partial_kernel(
    list_ref, q_ref, *refs, have, first, home, collect, heads, block, named, steps, group, factor,
):
    pieces = 1 + max(p for p, _ in home)
    parts, refs = refs[: 3 * pieces], refs[3 * pieces :]
    home = [(parts[3 * p : 3 * p + 3], i) for p, i in home]
    if collect:
        loads, (kv, out_ref, top_ref, sum_ref, slot_of) = refs[:have], refs[have:]
        for p in range(have):
            kv[p] = loads[p][...]
    else:
        kv, out_ref, top_ref, sum_ref, slot_of = refs
    lanes = q_ref.shape[3]
    half = ID_ROWS // 2
    for p in range(slot_of.shape[0]):
        slot_of[p] = -1
    for p in range(have):
        tag = kv[p, pl.ds(2 * heads * block, ID_ROWS), :].astype(jnp.float32)
        slot_of[(tag[:half] * 256.0 + tag[half:]).astype(jnp.int32)[0, 0]] = p
    which = lax.broadcasted_iota(jnp.int32, (1, named * block), 1) // block
    for o, ((near_out, near_top, near_sum), i) in enumerate(home):
        r = first + o
        spots = [slot_of[list_ref[j, r]] for j in range(named)]
        places = [jnp.maximum(x, 0) for x in spots]
        bias = jnp.zeros(which.shape, jnp.float32)
        for j in range(named):
            bias = jnp.where(which == j, jnp.where(spots[j] < 0, -jnp.inf, 0.0), bias)
        scores, values = [], []
        for g in range(heads):
            q = jnp.concatenate(
                [q_ref[r, s, g * group : (g + 1) * group, :] for s in range(steps)], axis=0
            )
            k = jnp.concatenate([kv[p, pl.ds(g * block, block), :] for p in places], axis=0)
            values.append(
                jnp.concatenate([kv[p, pl.ds((heads + g) * block, block), :] for p in places], axis=0)
            )
            scores.append(lax.dot_general(q, k, NT, preferred_element_type=jnp.float32) + bias)
        for g in range(heads):
            near = near_top[i, g]
            best = jnp.max(scores[g], axis=1, keepdims=True)
            top = jnp.maximum(near, jnp.broadcast_to(best, near.shape))
            w = [
                jnp.exp2((scores[g][:, c : c + lanes] - top) * factor)
                for c in range(0, named * block, lanes)
            ]
            keep = jnp.exp2((near - top) * factor)
            sum_ref[o, g] = near_sum[i, g] * keep + jnp.sum(sum(w[1:], w[0]), axis=1, keepdims=True)
            weights = jnp.concatenate([x.astype(jnp.bfloat16) for x in w], axis=1)
            out_ref[o, g] = near_out[i, g] * keep + jnp.dot(
                weights, values[g], preferred_element_type=jnp.float32
            )
            top_ref[o, g] = top


def final_kernel(list_ref, q_ref, *refs, spans, batch, heads, block, named, steps, group, factor):
    pieces = len(spans)
    parts, (one_ref, two_ref, out_hbm, out_ref, sems) = refs[: 3 * pieces], refs[3 * pieces :]
    home = [(parts[3 * p : 3 * p + 3], i) for p, (_, count) in enumerate(spans) for i in range(count)]
    half, rows = ID_ROWS // 2, steps * group
    loads = (one_ref, two_ref)
    numbers = []
    for load in loads:
        tag = load[pl.ds(2 * heads * block, ID_ROWS), :].astype(jnp.float32)
        numbers.append((tag[:half] * 256.0 + tag[half:]).astype(jnp.int32)[0, 0])
    which = lax.broadcasted_iota(jnp.int32, (1, 2 * block), 1) // block
    outs = []
    for start in range(0, len(home), batch):
        span = range(start, min(start + batch, len(home)))
        biases = []
        for r in span:
            bias = jnp.full(which.shape, -jnp.inf, jnp.float32)
            for b in range(2):
                asked = list_ref[0, r] == numbers[b]
                for j in range(1, named):
                    asked = jnp.logical_or(asked, list_ref[j, r] == numbers[b])
                bias = jnp.where(which == b, jnp.where(asked, 0.0, -jnp.inf), bias)
            biases.append(bias)
        for g in range(heads):
            k = jnp.concatenate([x[pl.ds(g * block, block), :] for x in loads], axis=0)
            v = jnp.concatenate([x[pl.ds((heads + g) * block, block), :] for x in loads], axis=0)
            q = jnp.concatenate(
                [q_ref[r, s, g * group : (g + 1) * group, :] for r in span for s in range(steps)], axis=0
            )
            scores = lax.dot_general(q, k, NT, preferred_element_type=jnp.float32)
            weights, keeps, totals = [], [], []
            for o, r in enumerate(span):
                (_, near_top, near_sum), i = home[r]
                near = near_top[i, g]
                own = scores[o * rows : (o + 1) * rows] + biases[o]
                best = jnp.max(own, axis=1, keepdims=True)
                top = jnp.maximum(near, jnp.broadcast_to(best, near.shape))
                w = jnp.exp2((own - top[:, :1] if top.shape[1] != own.shape[1] else own - top) * factor)
                keep = jnp.exp2((near - top) * factor)
                totals.append(near_sum[i, g] * keep + jnp.sum(w, axis=1, keepdims=True))
                weights.append(w.astype(jnp.bfloat16))
                keeps.append(keep)
            mixed = jnp.dot(jnp.concatenate(weights, axis=0), v, preferred_element_type=jnp.float32)
            for o, r in enumerate(span):
                (near_out, _, _), i = home[r]
                out = near_out[i, g] * keeps[o] + mixed[o * rows : (o + 1) * rows]
                out = (out / totals[o]).astype(out_ref.dtype)
                for s in range(steps):
                    out_ref[r, s, g * group : (g + 1) * group, :] = out[s * group : (s + 1) * group]
        for r in span:
            outs.append(pltpu.make_async_copy(out_ref.at[r], out_hbm.at[r], sems.at[r]))
            outs[-1].start()
    for c in outs:
        c.wait()


def per_device(
    queries, new_keys, new_values, suffix_keys, suffix_values, suffix_len,
    prefix_keys, prefix_values, block_ids, block_lists, *, devices, pieces=3,
):
    requests, steps, head_count, width = queries.shape
    heads = new_keys.shape[2]
    group = head_count // heads
    slots = suffix_keys.shape[1]
    block = prefix_keys.shape[1]
    named = block_lists.shape[1]
    factor = math.log2(math.e) / math.sqrt(width)
    rows = steps * group
    kind = queries.dtype
    far = pl.BlockSpec(memory_space=pltpu.HBM)
    vmem = pl.BlockSpec(memory_space=pltpu.VMEM)
    smem = pl.BlockSpec(memory_space=pltpu.SMEM)
    load_rows = 2 * heads * block + ID_ROWS
    tie = lambda *arrays: lax.optimization_barrier(arrays)
    away = functools.partial(pltpu.with_memory_space_constraint, memory_space=pltpu.HBM)
    near = functools.partial(pltpu.with_memory_space_constraint, memory_space=pltpu.VMEM)
    limit = lambda mib: pltpu.CompilerParams(vmem_limit_bytes=mib << 20)

    load = pl.pallas_call(
        functools.partial(pack_kernel, heads=heads, block=block),
        out_shape=pltpu.VMEM((load_rows, width), kind),
        in_specs=[smem, far, far],
        out_specs=vmem,
        scratch_shapes=[
            pltpu.VMEM((2, heads * block, width), kind),
            pltpu.VMEM((2, heads * block, width), jnp.float32),
            pltpu.SemaphoreType.DMA((2,)),
        ],
        compiler_params=limit(4),
        name="pack",
    )(
        block_ids,
        away(prefix_keys.reshape(heads * block, width)),
        away(prefix_values.reshape(heads * block, width)),
    )

    flat = [
        queries,
        new_keys.reshape(requests, steps * heads, width),
        new_values.reshape(requests, steps * heads, width),
        suffix_keys.reshape(requests, slots * heads, width),
        suffix_values.reshape(requests, slots * heads, width),
    ]
    sizes = [(requests + p) // pieces for p in range(pieces)][::-1]
    spans = [(sum(sizes[:p]), sizes[p]) for p in range(pieces)]

    def local(piece, lengths, arrays):
        first, count = spans[piece]
        fetch = piece == 0
        stats = [pltpu.VMEM((count, heads, rows, width), jnp.float32)] * 3
        handed = [pltpu.VMEM(x.shape, x.dtype) for x in arrays] if fetch else []
        return pl.pallas_call(
            functools.partial(
                local_kernel, first=first, count=count, fetch=fetch, heads=heads, steps=steps,
                group=group, factor=factor,
            ),
            out_shape=handed + stats,
            in_specs=[far] * 6 if fetch else [smem] + [vmem] * 5,
            out_specs=[vmem] * len(handed + stats),
            scratch_shapes=[pltpu.VMEM((2, slots * heads, width), jnp.float32)] * 2
            + [
                pltpu.SMEM((requests,), jnp.int32),
                pltpu.SemaphoreType.DMA,
                pltpu.SemaphoreType.DMA((requests, 5)),
            ][: 3 * fetch],
            compiler_params=limit(8),
        )(away(lengths) if fetch else lengths, *[(away if fetch else near)(x) for x in arrays])

    chips = devices // 2
    rounds = chips // 2
    if 2 <= chips <= 16 and chips % 2 == 0:
        ring = ring_of_chips(chips)
        ahead = [(2 * a + c, 2 * b + c) for a, b in zip(ring, ring[1:] + ring[:1]) for c in range(2)]
        back = [(b, a) for a, b in ahead]
        swap = [(d, d ^ 1) for d in range(devices)]
        send = lambda x, pairs: lax.ppermute(x, "loop", pairs)
        right = left = load
        loads, layout, held, parts, fresh = [load], [(0, 0)], [], [], []
        waiting = [load]

        for step in range(rounds):
            if step == 0:
                right, *flat = tie(load, *flat)
                left, lengths = right, suffix_len
            else:
                right, *fresh = tie(right, *fresh)
                lengths, left = tie(suffix_len, left)
                if step == 1:
                    held, fresh = fresh[:5], fresh[5:]
                parts += fresh
                fresh = []
            last = step == rounds - 1
            ahead_of = send(right, ahead)
            back_of = left if last else send(left, back)
            if step < pieces:
                fresh = local(step, lengths, held or flat)
            if last:
                for x in waiting:
                    layout.append((len(layout), 0))
                    loads.append(send(x, swap))
            right, left = ahead_of, back_of
            if not last:
                for x in (right, left):
                    layout.append((len(layout), 0))
                    loads.append(x)
                    waiting.append(x)
        if rounds == 1:
            held, fresh = fresh[:5], fresh[5:]
        parts += fresh
        lists = block_lists.T
        for piece in range(min(rounds, pieces), pieces):
            parts += local(piece, suffix_len, held)
        sizes = dict(heads=heads, block=block, named=named, steps=steps, group=group, factor=factor)

        where = [(p, i) for p, (_, n) in enumerate(spans) for i in range(n)]

        def partial(first, count, lists, sources, collect):
            home = where[first : first + count]
            low = home[0][0]
            near_parts = parts[3 * low : 3 * home[-1][0] + 3]
            home = [(p - low, i) for p, i in home]
            have = devices - 2
            stats = [pltpu.VMEM((count, heads, rows, width), jnp.float32)] * 3
            made = [pltpu.VMEM((have, load_rows, width), kind)] if collect else []
            return pl.pallas_call(
                functools.partial(
                    partial_kernel, have=have, first=first, home=home, collect=collect, **sizes
                ),
                out_shape=made + stats,
                in_specs=[smem] + [vmem] * (1 + len(near_parts) + len(sources)),
                out_specs=[vmem] * len(made + stats),
                scratch_shapes=[pltpu.SMEM((devices,), jnp.int32)],
                compiler_params=limit(4),
            )(lists, *[near(x) for x in (held[0], *near_parts, *sources)])

        split = requests // 2
        collected, *early = partial(0, split, lists, loads, True)
        right, *early = tie(right, *early)
        lists, right = tie(lists, right)
        other = send(right, swap)
        late = partial(split, requests - split, lists, [collected], False)
        groups = [(0, split), (split, requests - split)]
        return pl.pallas_call(
            functools.partial(final_kernel, spans=groups, batch=requests, **sizes),
            out_shape=jax.ShapeDtypeStruct(queries.shape, kind),
            in_specs=[smem] + [vmem] * 9,
            out_specs=far,
            scratch_shapes=[pltpu.VMEM(queries.shape, kind), pltpu.SemaphoreType.DMA((requests,))],
            compiler_params=limit(8),
            name="final",
        )(lists, *[near(x) for x in (held[0], *early, *late, right, other)])
    gathered = lax.all_gather(load, "loop", axis=0)
    *held, a, b, c = local(0, suffix_len, flat)
    parts = [a, b, c]
    loads, layout = [away(gathered)], [None]
    for piece in range(1, pieces):
        parts += local(piece, suffix_len, held)

    return pl.pallas_call(
        functools.partial(
            prior_kernel, blocks=devices, layout=layout, spans=spans, heads=heads, block=block, named=named,
            steps=steps, group=group, factor=factor,
        ),
        out_shape=jax.ShapeDtypeStruct(queries.shape, kind),
        in_specs=[smem] + [vmem] * (1 + 3 * pieces) + [far if x is None else vmem for x in layout],
        out_specs=far,
        scratch_shapes=[
            pltpu.VMEM((devices, load_rows, width), kind),
            pltpu.VMEM(queries.shape, kind),
            pltpu.SMEM((devices,), jnp.int32),
            pltpu.SemaphoreType.DMA((requests,)),
            pltpu.SemaphoreType.DMA,
        ],
        compiler_params=limit(24),
        name="prior",
    )(block_lists.T, near(held[0]), *[near(x) for x in parts], *loads)


def solution(mesh):
    split = ("groups", "loop")
    in_specs = tuple(
        P(split, *([None] * (rank - 1))) for rank in (4, 4, 4, 4, 4, 1, 4, 4, 1, 2)
    )

    def body(*arrays):
        return per_device(*arrays, devices=mesh.shape["loop"])

    return jax.shard_map(
        body, mesh=mesh, in_specs=in_specs, out_specs=P(split, None, None, None), check_vma=False
    )
```
